512 devices in a mesh: section: 32 (over z_hi, x, core), expert: 16 (over y, z_lo).
Axes of the slice: x: 4, y: 8, z: 8 (z_hi: 4, z_lo: 2; z = z_hi * 2 + z_lo), core: 2. Of those that a mesh axis runs over, the one named last changes fastest.
Arguments:
- forward_input: bfloat16 [32, 2048, 2048], P('section', 'expert'), may hold values from -6 to 6
- forward_routes: int32 [32, 2048, 8], P('section', 'expert'), may hold values from 0 to 127, as said below
- forward_shares: float32 [32, 2048, 8], P('section', 'expert'), may hold values from 0.1 to 1
- backward_input: bfloat16 [32, 2048, 2048], P('section', 'expert'), may hold values from -6 to 6
- backward_routes: int32 [32, 2048, 8], P('section', 'expert'), may hold values from 0 to 127, as said below
- backward_shares: float32 [32, 2048, 8], P('section', 'expert'), may hold values from 0.1 to 1
- output_grad: bfloat16 [32, 2048, 2048], P('section', 'expert'), may hold values from -6 to 6
- norm_gain: float32 [32, 2048], P('section'), may hold values from 0.5 to 1.5
- gate_weight: bfloat16 [32, 3072, 2048], P('section', 'expert'), may hold values from -0.125 to 0.125
- up_weight: bfloat16 [32, 3072, 2048], P('section', 'expert'), may hold values from -0.125 to 0.125
- down_weight: bfloat16 [32, 3072, 2048], P('section', 'expert'), may hold values from -0.15625 to 0.15625
Outputs:
- next_input: bfloat16 [32, 2048, 2048], P('section', 'expert')
- previous_gradient: bfloat16 [32, 2048, 2048], P('section', 'expert')
The draws below stay inside these ranges and needn't reach their ends.
Inputs may be any that keep to these rules, and one draw needn't show every extreme that they name: `forward_routes`: each token names 8 different experts. Among the 128 tokens of one device, at most 16 name any one expert below 2; in every draw some section has every device sending exactly 16 tokens to one expert below 2. `backward_routes`: as for forward_routes.
All inputs are finite; a program needn't handle non-finite values.
Results may differ from the reference program's by a relative error of at most 0.007.
Values may be sent and summed in bfloat16 or wider, within the bound.
A program may use at most 64 MiB of HBM per device.

```python
import math
import jax
import jax.numpy as jnp
from jax import lax

D = 2048
HIDDEN_SIZE = 1536
EXPERTS = 128
TOPK = 8
EF = 2
TOK_DEV = 128
CAP = 16
TOKENS = 2048
N_SECTION = 32
N_EXPERT = 16


def routes_for(key):
    keys = jax.random.split(key, 6)
    counts = jax.random.randint(keys[0], (N_SECTION, N_EXPERT, EF), CAP // 2, CAP + 1)
    full_section = jax.random.randint(keys[1], (), 0, N_SECTION)
    full_expert = jax.random.randint(keys[2], (), 0, EF)
    section_index = jnp.arange(N_SECTION)[:, None, None]
    expert_index = jnp.arange(EF)[None, None, :]
    counts = jnp.where((section_index == full_section) & (expert_index == full_expert), CAP, counts)
    scores = jax.random.randint(keys[3], (N_SECTION, N_EXPERT, EF, TOK_DEV), 0, 1 << 20) * TOK_DEV + jnp.arange(TOK_DEV)
    ranks = jnp.argsort(jnp.argsort(scores, axis=-1), axis=-1)
    member = ranks < counts[..., None]
    member = jnp.transpose(member, (0, 1, 3, 2)).reshape(N_SECTION, N_EXPERT * TOK_DEV, EF)
    other_scores = jax.random.randint(keys[4], (N_SECTION, N_EXPERT * TOK_DEV, EXPERTS - EF), 0, 1 << 16)
    other_scores = other_scores * (EXPERTS - EF) + jnp.arange(EXPERTS - EF)
    others = lax.top_k(other_scores, TOPK)[1] + EF
    running = jnp.cumsum(member.astype(jnp.int32), axis=-1)
    held = running[..., -1:]
    place = jnp.arange(TOPK)
    chosen = member[..., None, :] & (running[..., None, :] == place[:, None] + 1)
    hosted_at = jnp.sum(jnp.where(chosen, jnp.arange(EF), 0), axis=-1)
    routes = jnp.where(place < held, hosted_at, others)
    turn = jax.random.randint(keys[5], (N_SECTION, N_EXPERT * TOK_DEV, 1), 0, TOPK)
    return jnp.take_along_axis(routes, (place + turn) % TOPK, axis=-1).astype(jnp.int32)


def draw_forward_routes(key, part):
    return routes_for(jax.random.fold_in(key, 11))


def draw_backward_routes(key, part):
    return routes_for(jax.random.fold_in(key, 23))


def block_levels(own_key, extent, shards, smallest, high):
    def one(dim, parts):
        draws = jax.random.uniform(jax.random.fold_in(jax.random.fold_in(own_key, 6), dim), (parts,), jnp.float32, smallest / len(shards), high / len(shards))
        return jnp.repeat(jnp.exp(draws), extent[dim] // parts).reshape((-1,) + (1,) * (len(extent) - dim - 1))

    level = one(*shards[0])
    for cut in shards[1:]:
        level = level * one(*cut)
    return level


def centred(key, extent, deviation, most, pieces=(), held_as=jnp.bfloat16):
    array = deviation * jax.random.normal(key, extent, jnp.float32)
    if pieces:
        array = array * block_levels(key, extent, pieces, -0.22, 0.18)
    return jnp.clip(array, -most, most).astype(held_as)


def setup_inputs(seed: int = 0) -> dict:
    key_list = jax.random.split(jax.random.key(seed), 12)
    return {
        "forward_input": centred(key_list[0], (N_SECTION, TOKENS, D), 1.0, 6.0, ((0, 32), (1, 16))),
        "forward_routes": draw_forward_routes(jax.random.fold_in(key_list[11], 71), 0),
        "forward_shares": jnp.clip(jnp.exp(math.log(1.0) - 2.3025851 * jax.random.uniform(key_list[2], (N_SECTION, TOKENS, TOPK), jnp.float32) ** block_levels(key_list[2], (N_SECTION, TOKENS, TOPK), ((0, 32), (1, 16)), -0.2, 0.2)), 0.1, 1.0),
        "backward_input": centred(key_list[3], (N_SECTION, TOKENS, D), 1.0, 6.0, ((0, 32), (1, 16))),
        "backward_routes": draw_backward_routes(jax.random.fold_in(key_list[11], 71), 0),
        "backward_shares": jnp.clip(jnp.exp(math.log(1.0) - 2.3025851 * jax.random.uniform(key_list[5], (N_SECTION, TOKENS, TOPK), jnp.float32) ** block_levels(key_list[5], (N_SECTION, TOKENS, TOPK), ((0, 32), (1, 16)), -0.2, 0.2)), 0.1, 1.0),
        "output_grad": centred(key_list[6], (N_SECTION, TOKENS, D), 1.0, 6.0, ((0, 32), (1, 16))),
        "norm_gain": jnp.clip(1.0 + 0.1 * jax.random.normal(key_list[7], (N_SECTION, D), jnp.float32), 0.5, 1.5),
        "gate_weight": centred(key_list[8], (N_SECTION, EF * HIDDEN_SIZE, D), D ** -0.5, 0.125, ((0, 32), (1, 16))),
        "up_weight": centred(key_list[9], (N_SECTION, EF * HIDDEN_SIZE, D), D ** -0.5, 0.125, ((0, 32), (1, 16))),
        "down_weight": centred(key_list[10], (N_SECTION, EF * HIDDEN_SIZE, D), HIDDEN_SIZE ** -0.5, 0.15625, ((0, 32), (1, 16))),
    }


EPSILON = 1e-06

def route_tables(route_ids, shares):
    hosted = jnp.arange(EF, dtype=jnp.int32)
    match = route_ids[:, :, None] == hosted
    member = jnp.any(match, axis=1)
    weight = lax.optimization_barrier(jnp.sum(jnp.where(match, shares[:, :, None], 0.0), axis=1))
    member_int = member.astype(jnp.int32)
    rank = jnp.cumsum(member_int, axis=0) - member_int
    slots = jnp.arange(CAP, dtype=jnp.int32)
    placed = member.T[:, None, :] & (rank.T[:, None, :] == slots[None, :, None])
    table = placed.astype(jnp.float32)
    return (table, table * weight.T[:, None, :])

def normalize(rows, gain):
    values = rows.astype(jnp.float32)
    scale = lax.rsqrt(lax.optimization_barrier(jnp.mean(values * values, axis=-1, keepdims=True)) + EPSILON)
    unit = values * scale
    return (unit, scale, (unit * gain).astype(jnp.bfloat16))

def slice_forward(slots_in, gate_rows, up_rows, down_rows):
    gate = jnp.dot(slots_in, gate_rows.T, preferred_element_type=jnp.float32)
    upper = jnp.dot(slots_in, up_rows.T, preferred_element_type=jnp.float32)
    hidden = (jax.nn.silu(gate) * upper).astype(jnp.bfloat16)
    return jnp.dot(hidden, down_rows, preferred_element_type=jnp.float32).astype(jnp.bfloat16)

def slice_backward(slots_in, slot_grad, gate_rows, up_rows, down_rows):
    gate = jnp.dot(slots_in, gate_rows.T, preferred_element_type=jnp.float32)
    upper = jnp.dot(slots_in, up_rows.T, preferred_element_type=jnp.float32)
    sigma = jax.nn.sigmoid(gate)
    hidden_grad = jnp.dot(slot_grad, down_rows.T, preferred_element_type=jnp.float32)
    gate_grad = (hidden_grad * upper * sigma * (1.0 + gate * (1.0 - sigma))).astype(jnp.bfloat16)
    upper_grad = (hidden_grad * gate * sigma).astype(jnp.bfloat16)
    total = jnp.dot(gate_grad, gate_rows, preferred_element_type=jnp.float32)
    total = total + jnp.dot(upper_grad, up_rows, preferred_element_type=jnp.float32)
    return total.astype(jnp.bfloat16)

def to_slots(table, rows):
    blocks = rows.astype(jnp.float32).reshape(N_EXPERT, TOK_DEV, D)
    return jnp.einsum('nect,ntd->necd', table, blocks, precision=lax.Precision.HIGHEST).astype(jnp.bfloat16)

def one_section(operands):
    forward_rows, forward_ids, forward_weights, backward_rows, backward_ids, backward_weights, grad_rows, gain, gate_all, up_all, down_all = operands
    group = N_EXPERT // EF
    width = HIDDEN_SIZE * EF // N_EXPERT
    forward_unit, forward_scale, forward_normed = normalize(forward_rows, gain)
    backward_unit, backward_scale, backward_normed = normalize(backward_rows, gain)
    forward_table, forward_weighted = jax.vmap(route_tables)(forward_ids.reshape(N_EXPERT, TOK_DEV, TOPK), forward_weights.reshape(N_EXPERT, TOK_DEV, TOPK))
    backward_table, backward_weighted = jax.vmap(route_tables)(backward_ids.reshape(N_EXPERT, TOK_DEV, TOPK), backward_weights.reshape(N_EXPERT, TOK_DEV, TOPK))
    forward_slots = to_slots(forward_table, forward_normed)
    backward_slots = to_slots(backward_table, backward_normed)
    grad_slots = to_slots(backward_weighted, grad_rows)
    forward_out = []
    backward_out = []
    for expert in range(EF):
        slots_f = forward_slots[:, expert].reshape(N_EXPERT * CAP, D)
        slots_b = backward_slots[:, expert].reshape(N_EXPERT * CAP, D)
        slots_g = grad_slots[:, expert].reshape(N_EXPERT * CAP, D)
        total_f = jnp.zeros((N_EXPERT * CAP, D), jnp.float32)
        total_b = jnp.zeros((N_EXPERT * CAP, D), jnp.float32)
        for piece in range(group):
            start = (expert * group + piece) * width
            gate_rows = gate_all[start:start + width]
            up_rows = up_all[start:start + width]
            down_rows = down_all[start:start + width]
            total_f = total_f + slice_forward(slots_f, gate_rows, up_rows, down_rows).astype(jnp.float32)
            total_b = total_b + slice_backward(slots_b, slots_g, gate_rows, up_rows, down_rows).astype(jnp.float32)
        forward_out.append(total_f.reshape(N_EXPERT, CAP, D))
        backward_out.append(total_b.reshape(N_EXPERT, CAP, D))
    forward_result = jnp.stack(forward_out, axis=1)
    backward_result = jnp.stack(backward_out, axis=1)
    mixed = jnp.einsum('nect,necd->ntd', forward_weighted, forward_result, precision=lax.Precision.HIGHEST).reshape(TOKENS, D)
    next_rows = (forward_rows.astype(jnp.float32) + mixed).astype(jnp.bfloat16)
    normed_grad = jnp.einsum('nect,necd->ntd', backward_table, backward_result, precision=lax.Precision.HIGHEST).reshape(TOKENS, D)
    scaled = normed_grad * gain
    input_grad = backward_scale * (scaled - backward_unit * lax.optimization_barrier(jnp.mean(scaled * backward_unit, axis=-1, keepdims=True)))
    previous_rows = (grad_rows.astype(jnp.float32) + input_grad).astype(jnp.bfloat16)
    return (next_rows, previous_rows)

def reference(forward_input, forward_routes, forward_shares, backward_input, backward_routes, backward_shares, output_grad, norm_gain, gate_weight, up_weight, down_weight):
    next_rows, previous_rows = lax.map(one_section, (forward_input, forward_routes, forward_shares, backward_input, backward_routes, backward_shares, output_grad, norm_gain, gate_weight, up_weight, down_weight))
    return (jnp.roll(next_rows, 1, axis=0), jnp.roll(previous_rows, -1, axis=0))
```

```python
import jax
import jax.numpy as jnp
from jax import lax
from jax.experimental import pallas as pl
from jax.experimental.pallas import tpu as pltpu
from jax.sharding import PartitionSpec as P

EF = 2
CAP = 16
EPSILON = 1e-06
MESH = pl.DeviceIdType.MESH
F32 = jnp.float32
BF16 = jnp.bfloat16


def project(left, right):
    return lax.dot_general(
        left, right, (((1,), (1,)), ((), ())), preferred_element_type=F32
    )


def multiply(left, right):
    return jnp.dot(left, right, preferred_element_type=F32)


def slot_table(routes, shares):
    tokens = routes.shape[0]
    lane = lax.broadcasted_iota(jnp.int32, (tokens, 128), 1)
    member = jnp.zeros((tokens, 128), F32)
    weight = jnp.zeros((tokens, 128), F32)
    for e in range(EF):
        match = routes == e
        named = jnp.sum(jnp.where(match, 1.0, 0.0), axis=1, keepdims=True)
        share = jnp.sum(jnp.where(match, shares, 0.0), axis=1, keepdims=True)
        mine = (lane >= e * CAP) & (lane < (e + 1) * CAP)
        member = jnp.where(mine, named, member)
        weight = jnp.where(mine, share, weight)
    before = lax.broadcasted_iota(jnp.int32, (tokens, tokens), 0)
    other = lax.broadcasted_iota(jnp.int32, (tokens, tokens), 1)
    earlier = jnp.where(other < before, 1.0, 0.0).astype(BF16)
    rank = multiply(earlier, member.astype(BF16))
    slot = jnp.where(lane >= CAP, lane - CAP, lane).astype(F32)
    table = jnp.where((member > 0.5) & (rank == slot), 1.0, 0.0)
    turned = jnp.transpose(table)[: EF * CAP]
    share = jnp.sum(jnp.transpose(table * weight)[: EF * CAP], axis=1, keepdims=True)
    return table.astype(BF16), turned.astype(BF16), share


def inverse_norm(rows):
    return lax.rsqrt(jnp.mean(rows * rows, axis=-1, keepdims=True) + EPSILON)


def layer_kernel(
    shape,
    forward_hbm,
    forward_routes,
    forward_shares,
    backward_hbm,
    backward_routes,
    backward_shares,
    grad_hbm,
    gain_ref,
    gate_hbm,
    up_hbm,
    down_hbm,
    next_ref,
    previous_ref,
    rows,
    weights,
    mine,
    held,
    unit,
    scale,
    own,
    z_out,
    z_in,
    y_out,
    y_in,
    step_out,
    step_in,
    base,
    table_out,
    table_in,
    load_sem,
    y_send,
    y_recv,
    z_send,
    z_recv,
    cz_send,
    cz_recv,
    cy_send,
    cy_recv,
    base_send,
    base_recv,
    table_send,
    table_recv,
    step_send,
    step_recv,
):
    n_section, n_expert = shape
    n_y = n_expert // 2
    half = n_y // EF
    section = lax.axis_index("section")
    position = lax.axis_index("expert")
    y = position // 2
    plane = position % 2
    hosted = y // half
    following = (section + 1) % n_section
    preceding = (section + n_section - 1) % n_section
    partner = {"expert": y * 2 + (1 - plane)}

    def offset(k):
        d = k // 2 + 1
        return d + (k % 2) * (n_y - 2 * d)

    loads = [
        pltpu.make_async_copy(src, dst, load_sem.at[i])
        for i, (src, dst) in enumerate(
            (
                (forward_hbm, rows.at[0]),
                (backward_hbm, rows.at[1]),
                (grad_hbm, rows.at[2]),
                (gate_hbm, weights.at[0]),
                (up_hbm, weights.at[1]),
                (down_hbm, weights.at[2]),
            )
        )
    ]
    for load in loads:
        load.start()

    barrier = pltpu.get_barrier_semaphore()

    def greet(k, carry):
        pl.semaphore_signal(
            barrier,
            inc=1,
            device_id={"expert": ((y + offset(k)) % n_y) * 2 + plane},
            device_id_type=MESH,
        )
        return carry

    lax.fori_loop(0, n_y - 1, greet, 0)
    pl.semaphore_signal(barrier, inc=1, device_id=partner, device_id_type=MESH)
    for neighbour in (following, preceding):
        pl.semaphore_signal(
            barrier, inc=1, device_id={"section": neighbour}, device_id_type=MESH
        )
    pl.semaphore_wait(barrier, n_y + 2)

    def slots_to(t, k):
        there = (y + offset(k)) % n_y
        return pltpu.make_async_remote_copy(
            src_ref=mine.at[t, there // half],
            dst_ref=held.at[t, plane, y],
            send_sem=y_send.at[t, k],
            recv_sem=y_recv.at[t, y],
            device_id={"expert": there * 2 + plane},
            device_id_type=MESH,
        )

    def slots_from(t, k):
        there = (y + n_y - offset(k)) % n_y
        return there, pltpu.make_async_remote_copy(
            src_ref=held.at[t, plane, there],
            dst_ref=held.at[t, plane, there],
            send_sem=y_send.at[t, k],
            recv_sem=y_recv.at[t, there],
            device_id={"expert": there * 2 + plane},
            device_id_type=MESH,
        )

    def across(t, j):
        return pltpu.make_async_remote_copy(
            src_ref=held.at[t, plane, j],
            dst_ref=held.at[t, plane, j],
            send_sem=z_send.at[t, j],
            recv_sem=z_recv.at[t, j],
            device_id=partner,
            device_id_type=MESH,
        )

    def part_across(t, j):
        return pltpu.make_async_remote_copy(
            src_ref=z_out.at[t, j],
            dst_ref=z_in.at[t, j],
            send_sem=cz_send.at[t, j],
            recv_sem=cz_recv.at[t, j],
            device_id=partner,
            device_id_type=MESH,
        )

    def part_to(t, k):
        there = (y + offset(k)) % n_y
        return there, pltpu.make_async_remote_copy(
            src_ref=y_out.at[t, there],
            dst_ref=y_in.at[t, y],
            send_sem=cy_send.at[t, k],
            recv_sem=cy_recv.at[t, y],
            device_id={"expert": there * 2 + plane},
            device_id_type=MESH,
        )

    def part_from(t, k):
        there = (y + n_y - offset(k)) % n_y
        return pltpu.make_async_remote_copy(
            src_ref=y_in.at[t, there],
            dst_ref=y_in.at[t, there],
            send_sem=cy_send.at[t, k],
            recv_sem=cy_recv.at[t, there],
            device_id={"expert": there * 2 + plane},
            device_id_type=MESH,
        )

    to_section = (following, preceding)

    def base_copy(g):
        return pltpu.make_async_remote_copy(
            src_ref=rows.at[2 * g],
            dst_ref=base.at[g],
            send_sem=base_send.at[g],
            recv_sem=base_recv.at[g],
            device_id={"section": to_section[g]},
            device_id_type=MESH,
        )

    def table_copy(g):
        return pltpu.make_async_remote_copy(
            src_ref=table_out.at[g],
            dst_ref=table_in.at[g],
            send_sem=table_send.at[g],
            recv_sem=table_recv.at[g],
            device_id={"section": to_section[g]},
            device_id_type=MESH,
        )

    def step_copy(g):
        return pltpu.make_async_remote_copy(
            src_ref=step_out.at[g],
            dst_ref=step_in.at[g],
            send_sem=step_send.at[g],
            recv_sem=step_recv.at[g],
            device_id={"section": to_section[g]},
            device_id_type=MESH,
        )

    gain = gain_ref[...]

    def publish(t, values):
        values = values.astype(BF16)
        for e in range(EF):
            mine[t, e] = values[e * CAP : (e + 1) * CAP]
        held[t, plane, y] = mine[t, hosted]

        def send(k, carry):
            slots_to(t, k).start()
            return carry

        lax.fori_loop(0, n_y - 1, send, 0)
        across(t, y).start()

    table_f, turned_f, share_f = slot_table(forward_routes[...], forward_shares[...])
    table_out[0] = table_f
    loads[0].wait()
    slots = multiply(turned_f, rows[0])
    publish(0, slots * inverse_norm(slots) * gain)
    table_b, turned_b, share_b = slot_table(backward_routes[...], backward_shares[...])
    table_out[1] = table_b
    loads[1].wait()
    slots = multiply(turned_b, rows[1])
    inverse = inverse_norm(slots)
    slots = slots * inverse
    unit[...] = slots
    scale[...] = jnp.broadcast_to(inverse, scale.shape)
    publish(1, slots * gain)
    loads[2].wait()
    publish(2, multiply(turned_b, rows[2]) * share_b)
    for g in range(2):
        base_copy(g).start()
        table_copy(g).start()
    for load in loads[3:]:
        load.wait()

    def relay(t):
        def one(k, carry):
            j, copy = slots_from(t, k)
            copy.wait_recv()
            across(t, j).start()
            return carry

        lax.fori_loop(0, n_y - 1, one, 0)

    def arrived(t):
        def one(j, carry):
            pltpu.make_async_remote_copy(
                src_ref=held.at[t, 1 - plane, j],
                dst_ref=held.at[t, 1 - plane, j],
                send_sem=z_send.at[t, j],
                recv_sem=z_recv.at[t, j],
                device_id=partner,
                device_id_type=MESH,
            ).wait_recv()
            return carry

        lax.fori_loop(0, n_y, one, 0)

    def block(t, p):
        return held[t, p].reshape(n_y * CAP, held.shape[-1])

    def forward_part(p):
        slots = block(0, p)
        gate = project(slots, weights[0])
        upper = project(slots, weights[1])
        hidden = (gate * jax.nn.sigmoid(gate) * upper).astype(BF16)
        return multiply(hidden, weights[2])

    def backward_part(p):
        slots = block(1, p)
        gate = project(slots, weights[0])
        upper = project(slots, weights[1])
        sigma = jax.nn.sigmoid(gate)
        hidden_grad = project(block(2, p), weights[2])
        gate_grad = hidden_grad * upper * sigma * (1.0 + gate * (1.0 - sigma))
        upper_grad = hidden_grad * gate * sigma
        return multiply(gate_grad.astype(BF16), weights[0]) + multiply(
            upper_grad.astype(BF16), weights[1]
        )

    def to_partner(t, part):
        z_out[t] = part.astype(BF16).reshape(z_out.shape[1:])

        def one(j, carry):
            part_across(t, j).start()
            return carry

        lax.fori_loop(0, n_y, one, 0)

    def combine(t):
        def one(k, carry):
            j, copy = part_to(t, k)
            part_across(t, j).wait_recv()
            total = own[t, j] + z_in[t, j].astype(F32)
            y_out[t, j] = total.astype(BF16)
            copy.start()
            return carry

        lax.fori_loop(0, n_y - 1, one, 0)
        part_across(t, y).wait_recv()
        y_in[t, y] = (own[t, y] + z_in[t, y].astype(F32)).astype(BF16)

    def collect(t):
        def one(k, carry):
            part_from(t, k).wait_recv()
            return carry

        lax.fori_loop(0, n_y - 1, one, 0)
        return [
            sum(y_in[t, e * half + r].astype(F32) for r in range(half))
            for e in range(EF)
        ]

    relay(0)
    own[0] = forward_part(plane).reshape(own.shape[1:])
    arrived(0)
    to_partner(0, forward_part(1 - plane))
    relay(1)
    relay(2)
    own[1] = backward_part(plane).reshape(own.shape[1:])
    combine(0)
    arrived(1)
    arrived(2)
    to_partner(1, backward_part(1 - plane))

    for e, total in enumerate(collect(0)):
        at = pl.ds(e * CAP, CAP)
        step_out[0, at] = (total * share_f[e * CAP : (e + 1) * CAP]).astype(BF16)
    step_copy(0).start()
    combine(1)
    for e, total in enumerate(collect(1)):
        at = pl.ds(e * CAP, CAP)
        scaled = total * gain
        along = unit[at]
        lean = jnp.mean(scaled * along, axis=-1, keepdims=True)
        value = scale[at, :1] * (scaled - along * lean)
        step_out[1, at] = value.astype(BF16)
    step_copy(1).start()

    for g, out in enumerate((next_ref, previous_ref)):
        base_copy(g).wait_recv()
        table_copy(g).wait_recv()
        step_copy(g).wait_recv()
        change = multiply(table_in[g][:, : EF * CAP], step_in[g])
        out[...] = (base[g].astype(F32) + change).astype(BF16)

    for g in range(2):
        base_copy(g).wait_send()
        table_copy(g).wait_send()
        step_copy(g).wait_send()
    for t in range(3):

        def sent(k, carry):
            slots_to(t, k).wait_send()
            return carry

        def crossed(j, carry):
            across(t, j).wait_send()
            return carry

        lax.fori_loop(0, n_y - 1, sent, 0)
        lax.fori_loop(0, n_y, crossed, 0)
    for t in range(2):

        def sent_part(k, carry):
            part_to(t, k)[1].wait_send()
            return carry

        def crossed_part(j, carry):
            part_across(t, j).wait_send()
            return carry

        lax.fori_loop(0, n_y - 1, sent_part, 0)
        lax.fori_loop(0, n_y, crossed_part, 0)


def on_device(
    forward_input,
    forward_routes,
    forward_shares,
    backward_input,
    backward_routes,
    backward_shares,
    output_grad,
    norm_gain,
    gate_weight,
    up_weight,
    down_weight,
):
    shape = (lax.axis_size("section"), lax.axis_size("expert"))
    n_y = shape[1] // 2
    tokens, width = forward_input.shape[1:]
    hidden = gate_weight.shape[1]
    vmem = pl.BlockSpec(memory_space=pltpu.VMEM)
    hbm = pl.BlockSpec(memory_space=pl.ANY)
    dma = pltpu.SemaphoreType.DMA

    def kernel(*refs):
        layer_kernel(shape, *refs)

    out = jax.ShapeDtypeStruct((tokens, width), BF16)
    next_rows, previous_rows = pl.pallas_call(
        kernel,
        out_shape=(out, out),
        in_specs=[hbm, vmem, vmem, hbm, vmem, vmem, hbm, vmem, hbm, hbm, hbm],
        out_specs=(vmem, vmem),
        scratch_shapes=[
            pltpu.VMEM((3, tokens, width), BF16),
            pltpu.VMEM((3, hidden, width), BF16),
            pltpu.VMEM((3, EF, CAP, width), BF16),
            pltpu.VMEM((3, 2, n_y, CAP, width), BF16),
            pltpu.VMEM((EF * CAP, width), F32),
            pltpu.VMEM((EF * CAP, 128), F32),
            pltpu.VMEM((2, n_y, CAP, width), F32),
            pltpu.VMEM((2, n_y, CAP, width), BF16),
            pltpu.VMEM((2, n_y, CAP, width), BF16),
            pltpu.VMEM((2, n_y, CAP, width), BF16),
            pltpu.VMEM((2, n_y, CAP, width), BF16),
            pltpu.VMEM((2, EF * CAP, width), BF16),
            pltpu.VMEM((2, EF * CAP, width), BF16),
            pltpu.VMEM((2, tokens, width), BF16),
            pltpu.VMEM((2, tokens, 128), BF16),
            pltpu.VMEM((2, tokens, 128), BF16),
            dma((6,)),
            dma((3, n_y - 1)),
            dma((3, n_y)),
            dma((3, n_y)),
            dma((3, n_y)),
            dma((2, n_y)),
            dma((2, n_y)),
            dma((2, n_y - 1)),
            dma((2, n_y)),
            dma((2,)),
            dma((2,)),
            dma((2,)),
            dma((2,)),
            dma((2,)),
            dma((2,)),
        ],
        compiler_params=pltpu.CompilerParams(
            collective_id=0, has_side_effects=True, vmem_limit_bytes=48 << 20
        ),
    )(
        forward_input[0],
        forward_routes[0],
        forward_shares[0],
        backward_input[0],
        backward_routes[0],
        backward_shares[0],
        output_grad[0],
        norm_gain,
        gate_weight[0],
        up_weight[0],
        down_weight[0],
    )
    return next_rows[None], previous_rows[None]


def solution(mesh):
    rows = P("section", "expert", None)
    in_specs = (rows,) * 7 + (P("section", None),) + (rows,) * 3
    return jax.shard_map(
        on_device, mesh=mesh, in_specs=in_specs, out_specs=(rows, rows), check_vma=False
    )
```

```python
import jax
import jax.numpy as jnp
from jax import lax
from jax.experimental import pallas as pl
from jax.experimental.pallas import tpu as pltpu
from jax.sharding import PartitionSpec as P

EF = 2
CAP = 16
BATCHES = 4
OFFSETS = (0, 1, 7, 2, 6, 3, 5, 4)
EPSILON = 1e-06
MESH = pl.DeviceIdType.MESH
F32 = jnp.float32
BF16 = jnp.bfloat16


def project(left, right):
    return lax.dot_general(
        left, right, (((1,), (1,)), ((), ())), preferred_element_type=F32
    )


def multiply(left, right):
    return jnp.dot(left, right, preferred_element_type=F32)


def slot_table(routes, shares):
    tokens = routes.shape[1]
    slots = EF * CAP
    row = lax.broadcasted_iota(jnp.int32, (slots, tokens), 0)
    member = jnp.zeros((slots, tokens), F32)
    weight = jnp.zeros((slots, tokens), F32)
    for e in range(EF):
        match = routes == e
        named = jnp.sum(jnp.where(match, 1.0, 0.0), axis=0, keepdims=True)
        share = jnp.sum(jnp.where(match, shares, 0.0), axis=0, keepdims=True)
        mine = (row >= e * CAP) & (row < (e + 1) * CAP)
        member = jnp.where(mine, named, member)
        weight = jnp.where(mine, share, weight)
    other = lax.broadcasted_iota(jnp.int32, (tokens, tokens), 0)
    token = lax.broadcasted_iota(jnp.int32, (tokens, tokens), 1)
    earlier = jnp.where(other < token, 1.0, 0.0).astype(BF16)
    rank = multiply(member.astype(BF16), earlier)
    slot = jnp.where(row >= CAP, row - CAP, row).astype(F32)
    table = jnp.where((member > 0.5) & (rank == slot), 1.0, 0.0)
    share = jnp.sum(table * weight, axis=1, keepdims=True)
    return table.astype(BF16), share


def inverse_norm(rows):
    return lax.rsqrt(jnp.mean(rows * rows, axis=-1, keepdims=True) + EPSILON)


def layer_kernel(
    shape,
    forward_hbm,
    forward_routes_hbm,
    forward_shares_hbm,
    backward_hbm,
    backward_routes_hbm,
    backward_shares_hbm,
    grad_hbm,
    gain_hbm,
    gate_hbm,
    up_hbm,
    down_hbm,
    next_ref,
    previous_ref,
    rows,
    routes,
    shares,
    gain_ref,
    weights,
    mine,
    held,
    unit,
    scale,
    own,
    z_out,
    z_in,
    y_out,
    y_in,
    step_out,
    step_in,
    base,
    table_out,
    table_in,
    load_sem,
    y_send,
    y_recv,
    z_send,
    z_recv,
    cz_send,
    cz_recv,
    cy_send,
    cy_recv,
    base_send,
    base_recv,
    table_send,
    table_recv,
    step_send,
    step_recv,
):
    n_section, n_expert = shape
    n_y = n_expert // 2
    half = n_y // EF
    section = lax.axis_index("section")
    position = lax.axis_index("expert")
    y = position // 2
    plane = position % 2
    hosted = y // half
    following = (section + 1) % n_section
    preceding = (section + n_section - 1) % n_section
    partner = {"expert": y * 2 + (1 - plane)}

    offsets = OFFSETS
    self_k = offsets.index(0)
    rows_away = [k for k in range(n_y) if k != self_k]

    def row_to(k):
        return (y + offsets[k]) % n_y

    def row_from(k):
        return (y + n_y - offsets[k]) % n_y

    loads = [
        pltpu.make_async_copy(src, dst, load_sem.at[i])
        for i, (src, dst) in enumerate(
            (
                (forward_routes_hbm, routes.at[0]),
                (forward_shares_hbm, shares.at[0]),
                (forward_hbm, rows.at[0]),
                (gain_hbm, gain_ref),
                (backward_routes_hbm, routes.at[1]),
                (backward_shares_hbm, shares.at[1]),
                (backward_hbm, rows.at[1]),
                (grad_hbm, rows.at[2]),
                (gate_hbm, weights.at[0]),
                (up_hbm, weights.at[1]),
                (down_hbm, weights.at[2]),
            )
        )
    ]
    for load in loads:
        load.start()

    barrier = pltpu.get_barrier_semaphore()

    for k in rows_away:
        pl.semaphore_signal(
            barrier,
            inc=1,
            device_id={"expert": row_to(k) * 2 + plane},
            device_id_type=MESH,
        )
    pl.semaphore_signal(barrier, inc=1, device_id=partner, device_id_type=MESH)
    for neighbour in (following, preceding):
        pl.semaphore_signal(
            barrier, inc=1, device_id={"section": neighbour}, device_id_type=MESH
        )
    def slots_to(t, k):
        there = row_to(k)
        return pltpu.make_async_remote_copy(
            src_ref=mine.at[t, there // half],
            dst_ref=held.at[t, plane, k],
            send_sem=y_send.at[t, k],
            recv_sem=y_recv.at[t, k],
            device_id={"expert": there * 2 + plane},
            device_id_type=MESH,
        )

    def across(t, k):
        return pltpu.make_async_remote_copy(
            src_ref=held.at[t, plane, k],
            dst_ref=held.at[t, plane, k],
            send_sem=z_send.at[t, k],
            recv_sem=z_recv.at[t, k],
            device_id=partner,
            device_id_type=MESH,
        )

    def part_across(t, k):
        return pltpu.make_async_remote_copy(
            src_ref=z_out.at[t, k],
            dst_ref=z_in.at[t, k],
            send_sem=cz_send.at[t, k],
            recv_sem=cz_recv.at[t, k],
            device_id=partner,
            device_id_type=MESH,
        )

    def part_to(t, k):
        return pltpu.make_async_remote_copy(
            src_ref=y_out.at[t, k],
            dst_ref=y_in.at[t, y],
            send_sem=cy_send.at[t, k],
            recv_sem=cy_recv.at[t, k],
            device_id={"expert": row_from(k) * 2 + plane},
            device_id_type=MESH,
        )

    to_section = (following, preceding)

    def base_copy(g):
        return pltpu.make_async_remote_copy(
            src_ref=rows.at[2 * g],
            dst_ref=base.at[g],
            send_sem=base_send.at[g],
            recv_sem=base_recv.at[g],
            device_id={"section": to_section[g]},
            device_id_type=MESH,
        )

    def table_copy(g):
        return pltpu.make_async_remote_copy(
            src_ref=table_out.at[g],
            dst_ref=table_in.at[g],
            send_sem=table_send.at[g],
            recv_sem=table_recv.at[g],
            device_id={"section": to_section[g]},
            device_id_type=MESH,
        )

    def step_copy(g):
        return pltpu.make_async_remote_copy(
            src_ref=step_out.at[g],
            dst_ref=step_in.at[g],
            send_sem=step_send.at[g],
            recv_sem=step_recv.at[g],
            device_id={"section": to_section[g]},
            device_id_type=MESH,
        )

    def keep(t, values):
        values = values.astype(BF16)
        for e in range(EF):
            mine[t, e] = values[e * CAP : (e + 1) * CAP]
        held[t, plane, self_k] = mine[t, hosted]

    per = n_y // BATCHES
    batches = [range(b * per, (b + 1) * per) for b in range(BATCHES)]

    for load in loads[:4]:
        load.wait()
    gain = gain_ref[...]
    table_f, share_f = slot_table(routes[0], shares[0])
    slots = multiply(table_f, rows[0])
    keep(0, slots * inverse_norm(slots) * gain)
    pl.semaphore_wait(barrier, n_y + 2)
    across(0, self_k).start()
    for k in batches[0]:
        if k != self_k:
            slots_to(0, k).start()
    for load in loads[4:8]:
        load.wait()
    table_b, share_b = slot_table(routes[1], shares[1])
    slots = multiply(table_b, rows[1])
    inverse = inverse_norm(slots)
    slots = slots * inverse
    unit[...] = slots
    scale[...] = jnp.broadcast_to(inverse, scale.shape)
    keep(1, slots * gain)
    across(1, self_k).start()
    for k in batches[0]:
        if k != self_k:
            slots_to(1, k).start()
    keep(2, multiply(table_b, rows[2]) * share_b)
    across(2, self_k).start()
    for k in batches[0]:
        if k != self_k:
            slots_to(2, k).start()
    for batch in batches[1:]:
        for k in batch:
            if k != self_k:
                for t in range(3):
                    slots_to(t, k).start()
    for g, table in enumerate((table_f, table_b)):
        table_out[g] = table
        table_copy(g).start()
    for load in loads[8:]:
        load.wait()

    def relay(batch):
        for k in batch:
            if k != self_k:
                for t in range(3):
                    slots_to(t, k).wait_recv()
                    across(t, k).start()

    def arrived(t, batch):
        for k in batch:
            across(t, k).wait_recv()

    def block(t, batch):
        taken = held[t, :, batch[0] : batch[-1] + 1]
        return taken.reshape(2 * per * CAP, taken.shape[-1])

    def forward_part(batch):
        slots = block(0, batch)
        gate = project(slots, weights[0])
        upper = project(slots, weights[1])
        hidden = (gate * jax.nn.sigmoid(gate) * upper).astype(BF16)
        return multiply(hidden, weights[2])

    def backward_part(batch):
        slots = block(1, batch)
        gate = project(slots, weights[0])
        upper = project(slots, weights[1])
        sigma = jax.nn.sigmoid(gate)
        hidden_grad = project(block(2, batch), weights[2])
        gate_grad = hidden_grad * upper * sigma * (1.0 + gate * (1.0 - sigma))
        upper_grad = hidden_grad * gate * sigma
        return multiply(gate_grad.astype(BF16), weights[0]) + multiply(
            upper_grad.astype(BF16), weights[1]
        )

    def to_partner(t, batch, part):
        at = slice(batch[0], batch[-1] + 1)
        own[t, :, at] = part.reshape(2, per, CAP, part.shape[-1])
        for k in batch:
            z_out[t, k] = own[t, 1 - plane, k].astype(BF16)
            part_across(t, k).start()

    def compute(batch):
        arrived(0, batch)
        to_partner(0, batch, forward_part(batch))
        arrived(1, batch)
        arrived(2, batch)
        to_partner(1, batch, backward_part(batch))

    def combine(t, batch):
        for k in batch:
            part_across(t, k).wait_recv()
            total = (own[t, plane, k] + z_in[t, k].astype(F32)).astype(BF16)
            if k == self_k:
                y_in[t, y] = total
            else:
                y_out[t, k] = total
                part_to(t, k).start()

    def collect(t):
        for k in rows_away:
            part_to(t, k).wait_recv()
        return [
            sum(y_in[t, e * half + r].astype(F32) for r in range(half))
            for e in range(EF)
        ]

    relay(batches[0])
    for b, batch in enumerate(batches):
        if b + 1 < BATCHES:
            relay(batches[b + 1])
        compute(batch)
        if b:
            for t in range(2):
                combine(t, batches[b - 1])
    for g in range(2):
        base_copy(g).start()
    combine(0, batches[-1])
    combine(1, batches[-1])
    for e, total in enumerate(collect(0)):
        at = pl.ds(e * CAP, CAP)
        step_out[0, at] = (total * share_f[e * CAP : (e + 1) * CAP]).astype(BF16)
    step_copy(0).start()
    for e, total in enumerate(collect(1)):
        at = pl.ds(e * CAP, CAP)
        scaled = total * gain
        along = unit[at]
        lean = jnp.mean(scaled * along, axis=-1, keepdims=True)
        value = scale[at, :1] * (scaled - along * lean)
        step_out[1, at] = value.astype(BF16)
    step_copy(1).start()

    for g, out in enumerate((next_ref, previous_ref)):
        base_copy(g).wait_recv()
        table_copy(g).wait_recv()
        step_copy(g).wait_recv()
        change = lax.dot_general(
            table_in[g],
            step_in[g],
            (((0,), (0,)), ((), ())),
            preferred_element_type=F32,
        )
        out[...] = (base[g].astype(F32) + change).astype(BF16)

    for g in range(2):
        base_copy(g).wait_send()
        table_copy(g).wait_send()
        step_copy(g).wait_send()
    for t in range(3):
        for k in rows_away:
            slots_to(t, k).wait_send()
        for k in range(n_y):
            across(t, k).wait_send()
    for t in range(2):
        for k in rows_away:
            part_to(t, k).wait_send()
        for k in range(n_y):
            part_across(t, k).wait_send()


def on_device(
    forward_input,
    forward_routes,
    forward_shares,
    backward_input,
    backward_routes,
    backward_shares,
    output_grad,
    norm_gain,
    gate_weight,
    up_weight,
    down_weight,
):
    shape = (lax.axis_size("section"), lax.axis_size("expert"))
    n_y = shape[1] // 2
    tokens, width = forward_input.shape[1:]
    hidden = gate_weight.shape[1]
    topk = forward_routes.shape[2]
    vmem = pl.BlockSpec(memory_space=pltpu.VMEM)
    hbm = pl.BlockSpec(memory_space=pltpu.HBM)
    dma = pltpu.SemaphoreType.DMA

    def kernel(*refs):
        layer_kernel(shape, *refs)

    out = jax.ShapeDtypeStruct((tokens, width), BF16)
    next_rows, previous_rows = pl.pallas_call(
        kernel,
        out_shape=(out, out),
        in_specs=[hbm] * 11,
        out_specs=(vmem, vmem),
        scratch_shapes=[
            pltpu.VMEM((3, tokens, width), BF16),
            pltpu.VMEM((2, topk, tokens), jnp.int32),
            pltpu.VMEM((2, topk, tokens), F32),
            pltpu.VMEM((1, width), F32),
            pltpu.VMEM((3, hidden, width), BF16),
            pltpu.VMEM((3, EF, CAP, width), BF16),
            pltpu.VMEM((3, 2, n_y, CAP, width), BF16),
            pltpu.VMEM((EF * CAP, width), F32),
            pltpu.VMEM((EF * CAP, 128), F32),
            pltpu.VMEM((2, 2, n_y, CAP, width), F32),
            pltpu.VMEM((2, n_y, CAP, width), BF16),
            pltpu.VMEM((2, n_y, CAP, width), BF16),
            pltpu.VMEM((2, n_y, CAP, width), BF16),
            pltpu.VMEM((2, n_y, CAP, width), BF16),
            pltpu.VMEM((2, EF * CAP, width), BF16),
            pltpu.VMEM((2, EF * CAP, width), BF16),
            pltpu.VMEM((2, tokens, width), BF16),
            pltpu.VMEM((2, EF * CAP, tokens), BF16),
            pltpu.VMEM((2, EF * CAP, tokens), BF16),
            dma((11,)),
            dma((3, n_y)),
            dma((3, n_y)),
            dma((3, n_y)),
            dma((3, n_y)),
            dma((2, n_y)),
            dma((2, n_y)),
            dma((2, n_y)),
            dma((2, n_y)),
            dma((2,)),
            dma((2,)),
            dma((2,)),
            dma((2,)),
            dma((2,)),
            dma((2,)),
        ],
        compiler_params=pltpu.CompilerParams(
            collective_id=0, has_side_effects=True, vmem_limit_bytes=56 << 20
        ),
    )(
        forward_input[0],
        forward_routes[0].T,
        forward_shares[0].T,
        backward_input[0],
        backward_routes[0].T,
        backward_shares[0].T,
        output_grad[0],
        norm_gain,
        gate_weight[0],
        up_weight[0],
        down_weight[0],
    )
    return next_rows[None], previous_rows[None]


def solution(mesh):
    rows = P("section", "expert", None)
    in_specs = (rows,) * 7 + (P("section", None),) + (rows,) * 3
    return jax.shard_map(
        on_device, mesh=mesh, in_specs=in_specs, out_specs=(rows, rows), check_vma=False
    )
```

```python
import jax
import jax.numpy as jnp
from jax import lax
from jax.experimental import pallas as pl
from jax.experimental.pallas import tpu as pltpu
from jax.sharding import PartitionSpec as P

EF = 2
CAP = 16
PER_Z = 8
OFFSETS = (0, 1, 7, 2, 6, 3, 5, 4)
EPSILON = 1e-06
MESH = pl.DeviceIdType.MESH
F32 = jnp.float32
BF16 = jnp.bfloat16


def project(left, right):
    return lax.dot_general(
        left, right, (((1,), (1,)), ((), ())), preferred_element_type=F32
    )


def multiply(left, right):
    return jnp.dot(left, right, preferred_element_type=F32)


def slot_table(routes, shares):
    tokens = routes.shape[1]
    slots = EF * CAP
    row = lax.broadcasted_iota(jnp.int32, (slots, tokens), 0)
    member = jnp.zeros((slots, tokens), F32)
    weight = jnp.zeros((slots, tokens), F32)
    for e in range(EF):
        match = routes == e
        named = jnp.sum(jnp.where(match, 1.0, 0.0), axis=0, keepdims=True)
        share = jnp.sum(jnp.where(match, shares, 0.0), axis=0, keepdims=True)
        mine = (row >= e * CAP) & (row < (e + 1) * CAP)
        member = jnp.where(mine, named, member)
        weight = jnp.where(mine, share, weight)
    other = lax.broadcasted_iota(jnp.int32, (tokens, tokens), 0)
    token = lax.broadcasted_iota(jnp.int32, (tokens, tokens), 1)
    earlier = jnp.where(other < token, 1.0, 0.0).astype(BF16)
    rank = multiply(member.astype(BF16), earlier)
    slot = jnp.where(row >= CAP, row - CAP, row).astype(F32)
    table = jnp.where((member > 0.5) & (rank == slot), 1.0, 0.0)
    share = jnp.sum(table * weight, axis=1, keepdims=True)
    return table.astype(BF16), share


def inverse_norm(rows):
    return lax.rsqrt(jnp.mean(rows * rows, axis=-1, keepdims=True) + EPSILON)


def layer_kernel(
    shape,
    forward_hbm,
    forward_routes_hbm,
    forward_shares_hbm,
    backward_hbm,
    backward_routes_hbm,
    backward_shares_hbm,
    grad_hbm,
    gain_hbm,
    gate_hbm,
    up_hbm,
    down_hbm,
    next_ref,
    previous_ref,
    rows,
    routes,
    shares,
    gain_ref,
    weights,
    mine,
    held,
    unit,
    scale,
    own,
    z_out,
    z_in,
    y_out,
    y_in,
    step_out,
    step_in,
    base,
    stop,
    table_out,
    table_in,
    load_sem,
    y_send,
    y_recv,
    z_send,
    z_recv,
    cz_send,
    cz_recv,
    cy_send,
    cy_recv,
    base_send,
    base_recv,
    stop_send,
    stop_recv,
    table_send,
    table_recv,
    step_send,
    step_recv,
):
    n_section, n_expert = shape
    n_y = n_expert // 2
    half = n_y // EF
    section = lax.axis_index("section")
    position = lax.axis_index("expert")
    y = position // 2
    plane = position % 2
    hosted = y // half
    following = (section + 1) % n_section
    preceding = (section + n_section - 1) % n_section
    partner = {"expert": y * 2 + (1 - plane)}

    offsets = OFFSETS
    self_k = offsets.index(0)
    rows_away = [k for k in range(n_y) if k != self_k]

    def row_to(k):
        return (y + offsets[k]) % n_y

    def row_from(k):
        return (y + n_y - offsets[k]) % n_y

    loads = [
        pltpu.make_async_copy(src, dst, load_sem.at[i])
        for i, (src, dst) in enumerate(
            (
                (forward_routes_hbm, routes.at[0]),
                (forward_shares_hbm, shares.at[0]),
                (forward_hbm, rows.at[0]),
                (gain_hbm, gain_ref),
                (backward_routes_hbm, routes.at[1]),
                (backward_shares_hbm, shares.at[1]),
                (backward_hbm, rows.at[1]),
                (grad_hbm, rows.at[2]),
                (gate_hbm, weights.at[0]),
                (up_hbm, weights.at[1]),
                (down_hbm, weights.at[2]),
            )
        )
    ]
    barrier = pltpu.get_barrier_semaphore()

    for k in rows_away:
        pl.semaphore_signal(
            barrier,
            inc=1,
            device_id={"expert": row_to(k) * 2 + plane},
            device_id_type=MESH,
        )
    pl.semaphore_signal(barrier, inc=1, device_id=partner, device_id_type=MESH)
    for steps in (1, PER_Z - 2, PER_Z - 1, PER_Z):
        for way in (steps, n_section - steps):
            pl.semaphore_signal(
                barrier,
                inc=1,
                device_id={"section": (section + way) % n_section},
                device_id_type=MESH,
            )
    def slots_to(t, k):
        there = row_to(k)
        return pltpu.make_async_remote_copy(
            src_ref=mine.at[t, there // half],
            dst_ref=held.at[t, plane, k],
            send_sem=y_send.at[t, k],
            recv_sem=y_recv.at[t, k],
            device_id={"expert": there * 2 + plane},
            device_id_type=MESH,
        )

    def across(t, k):
        return pltpu.make_async_remote_copy(
            src_ref=held.at[t, plane, k],
            dst_ref=held.at[t, plane, k],
            send_sem=z_send.at[t, k],
            recv_sem=z_recv.at[t, k],
            device_id=partner,
            device_id_type=MESH,
        )

    def part_across(t, k):
        return pltpu.make_async_remote_copy(
            src_ref=z_out.at[t, k],
            dst_ref=z_in.at[t, k],
            send_sem=cz_send.at[t, k],
            recv_sem=cz_recv.at[t, k],
            device_id=partner,
            device_id_type=MESH,
        )

    def part_to(t, k):
        return pltpu.make_async_remote_copy(
            src_ref=y_out.at[t, k],
            dst_ref=y_in.at[t, y],
            send_sem=cy_send.at[t, k],
            recv_sem=cy_recv.at[t, k],
            device_id={"expert": row_from(k) * 2 + plane},
            device_id_type=MESH,
        )

    to_section = (following, preceding)

    spot = section % PER_Z
    turn = (1, -1)
    last = (spot == PER_Z - 1, spot == 0)
    between = ((spot == 1, spot == PER_Z - 1), (spot == PER_Z - 2, spot == 0))
    part_rows = rows.shape[1] // 2

    def section_at(steps):
        return {"section": (section + n_section + steps) % n_section}

    def base_half(g, h, src, steps):
        return pltpu.make_async_remote_copy(
            src_ref=src,
            dst_ref=base.at[g, pl.ds(h * part_rows, part_rows)],
            send_sem=base_send.at[g, h],
            recv_sem=base_recv.at[g, h],
            device_id=section_at(steps * turn[g]),
            device_id_type=MESH,
        )

    def base_copy(g, h):
        return base_half(g, h, rows.at[2 * g, pl.ds(h * part_rows, part_rows)], 1)

    def base_on(g, h):
        return base_half(g, h, stop.at[g, h], (PER_Z - 1, 1 - PER_Z)[h])

    def base_first(g, h):
        return pltpu.make_async_remote_copy(
            src_ref=rows.at[2 * g, pl.ds(h * part_rows, part_rows)],
            dst_ref=stop.at[g, h],
            send_sem=stop_send.at[g, h],
            recv_sem=stop_recv.at[g, h],
            device_id=section_at((2 - PER_Z, PER_Z)[h] * turn[g]),
            device_id_type=MESH,
        )

    halves = [(g, h) for g in range(2) for h in range(2)]

    def start_base():
        for g, h in halves:

            @pl.when(last[g])
            def _(g=g, h=h):
                base_first(g, h).start()

            @pl.when(jnp.logical_not(last[g]))
            def _(g=g, h=h):
                base_copy(g, h).start()

    def pass_base():
        for g, h in halves:

            @pl.when(between[g][h])
            def _(g=g, h=h):
                base_first(g, h).wait_recv()
                base_on(g, h).start()

    def end_base():
        for g, h in halves:

            @pl.when(last[g])
            def _(g=g, h=h):
                base_first(g, h).wait_send()

            @pl.when(jnp.logical_not(last[g]))
            def _(g=g, h=h):
                base_copy(g, h).wait_send()

            @pl.when(between[g][h])
            def _(g=g, h=h):
                base_on(g, h).wait_send()

    def table_copy(g):
        return pltpu.make_async_remote_copy(
            src_ref=table_out.at[g],
            dst_ref=table_in.at[g],
            send_sem=table_send.at[g],
            recv_sem=table_recv.at[g],
            device_id={"section": to_section[g]},
            device_id_type=MESH,
        )

    def step_copy(g):
        return pltpu.make_async_remote_copy(
            src_ref=step_out.at[g],
            dst_ref=step_in.at[g],
            send_sem=step_send.at[g],
            recv_sem=step_recv.at[g],
            device_id={"section": to_section[g]},
            device_id_type=MESH,
        )

    def keep(t, values):
        values = values.astype(BF16)
        for e in range(EF):
            mine[t, e] = values[e * CAP : (e + 1) * CAP]
        held[t, plane, self_k] = mine[t, hosted]

    for load in loads[:8]:
        load.start()

    def publish(t):
        across(t, self_k).start()
        for k in rows_away:
            slots_to(t, k).start()

    for load in loads[:4]:
        load.wait()
    gain = gain_ref[...]
    table_f, share_f = slot_table(routes[0], shares[0])
    slots = multiply(table_f, rows[0])
    keep(0, slots * inverse_norm(slots) * gain)
    pl.semaphore_wait(barrier, n_y + 8)
    publish(0)
    loads[7].wait()
    start_base()
    for load in loads[4:7]:
        load.wait()
    table_b, share_b = slot_table(routes[1], shares[1])
    slots = multiply(table_b, rows[1])
    inverse = inverse_norm(slots)
    slots = slots * inverse
    unit[...] = slots
    scale[...] = jnp.broadcast_to(inverse, scale.shape)
    keep(1, slots * gain)
    publish(1)
    keep(2, multiply(table_b, rows[2]) * share_b)
    publish(2)
    for load in loads[8:]:
        load.start()
    for g, table in enumerate((table_f, table_b)):
        table_out[g] = table
        table_copy(g).start()
    def relay(t):
        for k in rows_away:
            slots_to(t, k).wait_recv()
            across(t, k).start()

    def arrived(t, batch):
        for k in batch:
            across(t, k).wait_recv()

    def block(t, batch):
        taken = held[t, :, batch[0] : batch[-1] + 1]
        return taken.reshape(2 * len(batch) * CAP, taken.shape[-1])

    def forward_part(batch):
        slots = block(0, batch)
        gate = project(slots, weights[0])
        upper = project(slots, weights[1])
        hidden = (gate * jax.nn.sigmoid(gate) * upper).astype(BF16)
        return multiply(hidden, weights[2])

    def backward_part(batch):
        slots = block(1, batch)
        gate = project(slots, weights[0])
        upper = project(slots, weights[1])
        sigma = jax.nn.sigmoid(gate)
        hidden_grad = project(block(2, batch), weights[2])
        gate_grad = hidden_grad * upper * sigma * (1.0 + gate * (1.0 - sigma))
        upper_grad = hidden_grad * gate * sigma
        return multiply(gate_grad.astype(BF16), weights[0]) + multiply(
            upper_grad.astype(BF16), weights[1]
        )

    def to_partner(t, batch, part):
        own[t, :, batch[0] : batch[-1] + 1] = part.reshape(
            2, len(batch), CAP, part.shape[-1]
        )
        for k in reversed(batch):
            z_out[t, k] = own[t, 1 - plane, k].astype(BF16)
            part_across(t, k).start()

    def combine(t, batch):
        for k in reversed(batch):
            part_across(t, k).wait_recv()
            total = (own[t, plane, k] + z_in[t, k].astype(F32)).astype(BF16)
            if k == self_k:
                y_in[t, y] = total
            else:
                y_out[t, k] = total
                part_to(t, k).start()

    def collect(t):
        for k in rows_away:
            part_to(t, k).wait_recv()
        return [
            sum(y_in[t, e * half + r].astype(F32) for r in range(half))
            for e in range(EF)
        ]

    near = range(n_y // 2)
    far = range(n_y // 2, n_y)
    pass_base()
    relay(0)
    relay(1)
    arrived(0, range(n_y))
    for load in loads[8:]:
        load.wait()
    own_f = forward_part(range(n_y))
    relay(2)
    to_partner(0, range(n_y), own_f)
    arrived(1, range(n_y))
    arrived(2, far)
    to_partner(1, far, backward_part(far))
    combine(0, far)
    arrived(2, near)
    to_partner(1, near, backward_part(near))
    combine(0, near)
    combine(1, far)
    combine(1, near)
    for e, total in enumerate(collect(0)):
        at = pl.ds(e * CAP, CAP)
        step_out[0, at] = (total * share_f[e * CAP : (e + 1) * CAP]).astype(BF16)
    step_copy(0).start()
    for e, total in enumerate(collect(1)):
        at = pl.ds(e * CAP, CAP)
        scaled = total * gain
        along = unit[at]
        lean = jnp.mean(scaled * along, axis=-1, keepdims=True)
        value = scale[at, :1] * (scaled - along * lean)
        step_out[1, at] = value.astype(BF16)
    step_copy(1).start()

    for g, out in enumerate((next_ref, previous_ref)):
        for h in range(2):
            base_copy(g, h).wait_recv()
        table_copy(g).wait_recv()
        step_copy(g).wait_recv()
        change = lax.dot_general(
            table_in[g],
            step_in[g],
            (((0,), (0,)), ((), ())),
            preferred_element_type=F32,
        )
        out[...] = (base[g].astype(F32) + change).astype(BF16)

    for g in range(2):
        table_copy(g).wait_send()
        step_copy(g).wait_send()
    end_base()
    for t in range(3):
        for k in rows_away:
            slots_to(t, k).wait_send()
        for k in range(n_y):
            across(t, k).wait_send()
    for t in range(2):
        for k in rows_away:
            part_to(t, k).wait_send()
        for k in range(n_y):
            part_across(t, k).wait_send()


def on_device(
    forward_input,
    forward_routes,
    forward_shares,
    backward_input,
    backward_routes,
    backward_shares,
    output_grad,
    norm_gain,
    gate_weight,
    up_weight,
    down_weight,
):
    shape = (lax.axis_size("section"), lax.axis_size("expert"))
    n_y = shape[1] // 2
    tokens, width = forward_input.shape[1:]
    hidden = gate_weight.shape[1]
    topk = forward_routes.shape[2]
    vmem = pl.BlockSpec(memory_space=pltpu.VMEM)
    hbm = pl.BlockSpec(memory_space=pltpu.HBM)
    dma = pltpu.SemaphoreType.DMA

    def kernel(*refs):
        layer_kernel(shape, *refs)

    out = jax.ShapeDtypeStruct((tokens, width), BF16)
    next_rows, previous_rows = pl.pallas_call(
        kernel,
        out_shape=(out, out),
        in_specs=[hbm] * 11,
        out_specs=(vmem, vmem),
        scratch_shapes=[
            pltpu.VMEM((3, tokens, width), BF16),
            pltpu.VMEM((2, topk, tokens), jnp.int32),
            pltpu.VMEM((2, topk, tokens), F32),
            pltpu.VMEM((1, width), F32),
            pltpu.VMEM((3, hidden, width), BF16),
            pltpu.VMEM((3, EF, CAP, width), BF16),
            pltpu.VMEM((3, 2, n_y, CAP, width), BF16),
            pltpu.VMEM((EF * CAP, width), F32),
            pltpu.VMEM((EF * CAP, 128), F32),
            pltpu.VMEM((2, 2, n_y, CAP, width), F32),
            pltpu.VMEM((2, n_y, CAP, width), BF16),
            pltpu.VMEM((2, n_y, CAP, width), BF16),
            pltpu.VMEM((2, n_y, CAP, width), BF16),
            pltpu.VMEM((2, n_y, CAP, width), BF16),
            pltpu.VMEM((2, EF * CAP, width), BF16),
            pltpu.VMEM((2, EF * CAP, width), BF16),
            pltpu.VMEM((2, tokens, width), BF16),
            pltpu.VMEM((2, 2, tokens // 2, width), BF16),
            pltpu.VMEM((2, EF * CAP, tokens), BF16),
            pltpu.VMEM((2, EF * CAP, tokens), BF16),
            dma((11,)),
            dma((3, n_y)),
            dma((3, n_y)),
            dma((3, n_y)),
            dma((3, n_y)),
            dma((2, n_y)),
            dma((2, n_y)),
            dma((2, n_y)),
            dma((2, n_y)),
            dma((2, 2)),
            dma((2, 2)),
            dma((2, 2)),
            dma((2, 2)),
            dma((2,)),
            dma((2,)),
            dma((2,)),
            dma((2,)),
        ],
        compiler_params=pltpu.CompilerParams(
            collective_id=0, has_side_effects=True, vmem_limit_bytes=56 << 20
        ),
    )(
        forward_input[0],
        forward_routes[0].T,
        forward_shares[0].T,
        backward_input[0],
        backward_routes[0].T,
        backward_shares[0].T,
        output_grad[0],
        norm_gain,
        gate_weight[0],
        up_weight[0],
        down_weight[0],
    )
    return next_rows[None], previous_rows[None]


def solution(mesh):
    rows = P("section", "expert", None)
    in_specs = (rows,) * 7 + (P("section", None),) + (rows,) * 3
    return jax.shard_map(
        on_device, mesh=mesh, in_specs=in_specs, out_specs=(rows, rows), check_vma=False
    )
```

```python
import jax
import jax.numpy as jnp
from jax import lax
from jax.experimental import pallas as pl
from jax.experimental.pallas import tpu as pltpu
from jax.sharding import PartitionSpec as P

EF = 2
CAP = 16
PER_Z = 8
OFFSETS = (0, 7, 1, 2, 6, 4, 3, 5)
EPSILON = 1e-06
MESH = pl.DeviceIdType.MESH
F32 = jnp.float32
BF16 = jnp.bfloat16


def project(left, right):
    return lax.dot_general(
        left, right, (((1,), (1,)), ((), ())), preferred_element_type=F32
    )


def multiply(left, right):
    return jnp.dot(left, right, preferred_element_type=F32)


def slot_table(routes, shares):
    tokens = routes.shape[1]
    slots = EF * CAP
    row = lax.broadcasted_iota(jnp.int32, (slots, tokens), 0)
    member = jnp.zeros((slots, tokens), F32)
    weight = jnp.zeros((slots, tokens), F32)
    for e in range(EF):
        match = routes == e
        named = jnp.sum(jnp.where(match, 1.0, 0.0), axis=0, keepdims=True)
        share = jnp.sum(jnp.where(match, shares, 0.0), axis=0, keepdims=True)
        mine = (row >= e * CAP) & (row < (e + 1) * CAP)
        member = jnp.where(mine, named, member)
        weight = jnp.where(mine, share, weight)
    other = lax.broadcasted_iota(jnp.int32, (tokens, tokens), 0)
    token = lax.broadcasted_iota(jnp.int32, (tokens, tokens), 1)
    earlier = jnp.where(other < token, 1.0, 0.0).astype(BF16)
    rank = multiply(member.astype(BF16), earlier)
    slot = jnp.where(row >= CAP, row - CAP, row).astype(F32)
    table = jnp.where((member > 0.5) & (rank == slot), 1.0, 0.0)
    share = jnp.sum(table * weight, axis=1, keepdims=True)
    return table.astype(BF16), share


def inverse_norm(rows):
    return lax.rsqrt(jnp.mean(rows * rows, axis=-1, keepdims=True) + EPSILON)


def layer_kernel(
    shape,
    forward_hbm,
    forward_routes_hbm,
    forward_shares_hbm,
    backward_hbm,
    backward_routes_hbm,
    backward_shares_hbm,
    grad_hbm,
    gain_hbm,
    gate_hbm,
    up_hbm,
    down_hbm,
    next_ref,
    previous_ref,
    rows,
    routes,
    shares,
    gain_ref,
    weights,
    mine,
    held,
    unit,
    scale,
    own,
    z_out,
    z_in,
    y_out,
    y_in,
    step_out,
    step_in,
    base,
    stop,
    table_out,
    table_in,
    load_sem,
    y_send,
    y_recv,
    z_send,
    z_recv,
    cz_send,
    cz_recv,
    cy_send,
    cy_recv,
    base_send,
    base_recv,
    stop_send,
    stop_recv,
    table_send,
    table_recv,
    step_send,
    step_recv,
):
    n_section, n_expert = shape
    n_y = n_expert // 2
    half = n_y // EF
    section = lax.axis_index("section")
    position = lax.axis_index("expert")
    y = position // 2
    plane = position % 2
    hosted = y // half
    following = (section + 1) % n_section
    preceding = (section + n_section - 1) % n_section
    partner = {"expert": y * 2 + (1 - plane)}

    offsets = OFFSETS
    self_k = offsets.index(0)
    rows_away = [k for k in range(n_y) if k != self_k]

    def row_to(k):
        return (y + offsets[k]) % n_y

    def row_from(k):
        return (y + n_y - offsets[k]) % n_y

    loads = [
        pltpu.make_async_copy(src, dst, load_sem.at[i])
        for i, (src, dst) in enumerate(
            (
                (forward_routes_hbm, routes.at[0]),
                (forward_shares_hbm, shares.at[0]),
                (forward_hbm, rows.at[0]),
                (gain_hbm, gain_ref),
                (backward_routes_hbm, routes.at[1]),
                (backward_shares_hbm, shares.at[1]),
                (backward_hbm, rows.at[1]),
                (grad_hbm, rows.at[2]),
                (gate_hbm, weights.at[0]),
                (up_hbm, weights.at[1]),
                (down_hbm, weights.at[2]),
            )
        )
    ]
    barrier = pltpu.get_barrier_semaphore()

    for k in rows_away:
        pl.semaphore_signal(
            barrier,
            inc=1,
            device_id={"expert": row_to(k) * 2 + plane},
            device_id_type=MESH,
        )
    pl.semaphore_signal(barrier, inc=1, device_id=partner, device_id_type=MESH)
    for steps in (1, PER_Z - 2, PER_Z - 1, PER_Z):
        for way in (steps, n_section - steps):
            pl.semaphore_signal(
                barrier,
                inc=1,
                device_id={"section": (section + way) % n_section},
                device_id_type=MESH,
            )
    def slots_to(t, k):
        there = row_to(k)
        return pltpu.make_async_remote_copy(
            src_ref=mine.at[t, there // half],
            dst_ref=held.at[t, plane, k],
            send_sem=y_send.at[t, k],
            recv_sem=y_recv.at[t, k],
            device_id={"expert": there * 2 + plane},
            device_id_type=MESH,
        )

    def across(t, k):
        return pltpu.make_async_remote_copy(
            src_ref=held.at[t, plane, k],
            dst_ref=held.at[t, plane, k],
            send_sem=z_send.at[t, k],
            recv_sem=z_recv.at[t, k],
            device_id=partner,
            device_id_type=MESH,
        )

    def part_across(t, k):
        return pltpu.make_async_remote_copy(
            src_ref=z_out.at[t, k],
            dst_ref=z_in.at[t, k],
            send_sem=cz_send.at[t, k],
            recv_sem=cz_recv.at[t, k],
            device_id=partner,
            device_id_type=MESH,
        )

    def part_to(t, k):
        return pltpu.make_async_remote_copy(
            src_ref=y_out.at[t, k],
            dst_ref=y_in.at[t, y],
            send_sem=cy_send.at[t, k],
            recv_sem=cy_recv.at[t, k],
            device_id={"expert": row_from(k) * 2 + plane},
            device_id_type=MESH,
        )

    to_section = (following, preceding)

    spot = section % PER_Z
    turn = (1, -1)
    last = (spot == PER_Z - 1, spot == 0)
    between = ((spot == 1, spot == PER_Z - 1), (spot == PER_Z - 2, spot == 0))
    part_rows = rows.shape[1] // 2

    def section_at(steps):
        return {"section": (section + n_section + steps) % n_section}

    def base_half(g, h, src, steps):
        return pltpu.make_async_remote_copy(
            src_ref=src,
            dst_ref=base.at[g, pl.ds(h * part_rows, part_rows)],
            send_sem=base_send.at[g, h],
            recv_sem=base_recv.at[g, h],
            device_id=section_at(steps * turn[g]),
            device_id_type=MESH,
        )

    def base_copy(g, h):
        return base_half(g, h, rows.at[2 * g, pl.ds(h * part_rows, part_rows)], 1)

    def base_on(g, h):
        return base_half(g, h, stop.at[g, h], (PER_Z - 1, 1 - PER_Z)[h])

    def base_first(g, h):
        return pltpu.make_async_remote_copy(
            src_ref=rows.at[2 * g, pl.ds(h * part_rows, part_rows)],
            dst_ref=stop.at[g, h],
            send_sem=stop_send.at[g, h],
            recv_sem=stop_recv.at[g, h],
            device_id=section_at((2 - PER_Z, PER_Z)[h] * turn[g]),
            device_id_type=MESH,
        )

    halves = [(g, h) for g in range(2) for h in range(2)]

    def start_base():
        for g, h in halves:

            @pl.when(last[g])
            def _(g=g, h=h):
                base_first(g, h).start()

            @pl.when(jnp.logical_not(last[g]))
            def _(g=g, h=h):
                base_copy(g, h).start()

    def pass_base():
        for g, h in halves:

            @pl.when(between[g][h])
            def _(g=g, h=h):
                base_first(g, h).wait_recv()
                base_on(g, h).start()

    def end_base():
        for g, h in halves:

            @pl.when(last[g])
            def _(g=g, h=h):
                base_first(g, h).wait_send()

            @pl.when(jnp.logical_not(last[g]))
            def _(g=g, h=h):
                base_copy(g, h).wait_send()

            @pl.when(between[g][h])
            def _(g=g, h=h):
                base_on(g, h).wait_send()

    def table_copy(g):
        return pltpu.make_async_remote_copy(
            src_ref=table_out.at[g],
            dst_ref=table_in.at[g],
            send_sem=table_send.at[g],
            recv_sem=table_recv.at[g],
            device_id={"section": to_section[g]},
            device_id_type=MESH,
        )

    def step_copy(g):
        return pltpu.make_async_remote_copy(
            src_ref=step_out.at[g],
            dst_ref=step_in.at[g],
            send_sem=step_send.at[g],
            recv_sem=step_recv.at[g],
            device_id={"section": to_section[g]},
            device_id_type=MESH,
        )

    def keep(t, values):
        values = values.astype(BF16)
        for e in range(EF):
            mine[t, e] = values[e * CAP : (e + 1) * CAP]
        held[t, plane, self_k] = mine[t, hosted]

    for load in loads[:8]:
        load.start()

    def publish(t):
        across(t, self_k).start()
        for k in rows_away:
            slots_to(t, k).start()

    for load in loads[:4]:
        load.wait()
    gain = gain_ref[...]
    table_f, share_f = slot_table(routes[0], shares[0])
    slots = multiply(table_f, rows[0])
    keep(0, slots * inverse_norm(slots) * gain)
    pl.semaphore_wait(barrier, n_y + 8)
    publish(0)
    loads[7].wait()
    start_base()
    for load in loads[4:7]:
        load.wait()
    table_b, share_b = slot_table(routes[1], shares[1])
    slots = multiply(table_b, rows[1])
    inverse = inverse_norm(slots)
    slots = slots * inverse
    unit[...] = slots
    scale[...] = jnp.broadcast_to(inverse, scale.shape)
    keep(1, slots * gain)
    publish(1)
    keep(2, multiply(table_b, rows[2]) * share_b)
    publish(2)
    for load in loads[8:]:
        load.start()
    for g, table in enumerate((table_f, table_b)):
        table_out[g] = table
        table_copy(g).start()
    def relay(t):
        for k in rows_away:
            slots_to(t, k).wait_recv()
            across(t, k).start()

    def arrived(t, batch):
        for k in batch:
            across(t, k).wait_recv()

    def block(t, batch):
        taken = held[t, :, batch[0] : batch[-1] + 1]
        return taken.reshape(2 * len(batch) * CAP, taken.shape[-1])

    def forward_part(batch):
        slots = block(0, batch)
        gate = project(slots, weights[0])
        upper = project(slots, weights[1])
        hidden = (gate * jax.nn.sigmoid(gate) * upper).astype(BF16)
        return multiply(hidden, weights[2])

    def backward_part(batch):
        slots = block(1, batch)
        gate = project(slots, weights[0])
        upper = project(slots, weights[1])
        sigma = jax.nn.sigmoid(gate)
        hidden_grad = project(block(2, batch), weights[2])
        gate_grad = hidden_grad * upper * sigma * (1.0 + gate * (1.0 - sigma))
        upper_grad = hidden_grad * gate * sigma
        return multiply(gate_grad.astype(BF16), weights[0]) + multiply(
            upper_grad.astype(BF16), weights[1]
        )

    def to_partner(t, batch, part):
        own[t, :, batch[0] : batch[-1] + 1] = part.reshape(
            2, len(batch), CAP, part.shape[-1]
        )
        for k in reversed(batch):
            z_out[t, k] = own[t, 1 - plane, k].astype(BF16)
            part_across(t, k).start()

    def combine(t, batch):
        for k in reversed(batch):
            part_across(t, k).wait_recv()
            total = (own[t, plane, k] + z_in[t, k].astype(F32)).astype(BF16)
            if k == self_k:
                y_in[t, y] = total
            else:
                y_out[t, k] = total
                part_to(t, k).start()

    def collect(t):
        for k in rows_away:
            part_to(t, k).wait_recv()
        return [
            sum(y_in[t, e * half + r].astype(F32) for r in range(half))
            for e in range(EF)
        ]

    near = range(n_y // 2)
    far = range(n_y // 2, n_y)
    pass_base()
    relay(0)
    relay(1)
    arrived(0, range(n_y))
    for load in loads[8:]:
        load.wait()
    own_f = forward_part(range(n_y))
    relay(2)
    to_partner(0, range(n_y), own_f)
    arrived(1, range(n_y))
    arrived(2, far)
    to_partner(1, far, backward_part(far))
    combine(0, far)
    arrived(2, near)
    to_partner(1, near, backward_part(near))
    combine(0, near)
    combine(1, far)
    combine(1, near)
    for e, total in enumerate(collect(0)):
        at = pl.ds(e * CAP, CAP)
        step_out[0, at] = (total * share_f[e * CAP : (e + 1) * CAP]).astype(BF16)
    step_copy(0).start()
    for e, total in enumerate(collect(1)):
        at = pl.ds(e * CAP, CAP)
        scaled = total * gain
        along = unit[at]
        lean = jnp.mean(scaled * along, axis=-1, keepdims=True)
        value = scale[at, :1] * (scaled - along * lean)
        step_out[1, at] = value.astype(BF16)
    step_copy(1).start()

    for g, out in enumerate((next_ref, previous_ref)):
        for h in range(2):
            base_copy(g, h).wait_recv()
        table_copy(g).wait_recv()
        step_copy(g).wait_recv()
        change = lax.dot_general(
            table_in[g],
            step_in[g],
            (((0,), (0,)), ((), ())),
            preferred_element_type=F32,
        )
        out[...] = (base[g].astype(F32) + change).astype(BF16)

    for g in range(2):
        table_copy(g).wait_send()
        step_copy(g).wait_send()
    end_base()
    for t in range(3):
        for k in rows_away:
            slots_to(t, k).wait_send()
        for k in range(n_y):
            across(t, k).wait_send()
    for t in range(2):
        for k in rows_away:
            part_to(t, k).wait_send()
        for k in range(n_y):
            part_across(t, k).wait_send()


def on_device(
    forward_input,
    forward_routes,
    forward_shares,
    backward_input,
    backward_routes,
    backward_shares,
    output_grad,
    norm_gain,
    gate_weight,
    up_weight,
    down_weight,
):
    shape = (lax.axis_size("section"), lax.axis_size("expert"))
    n_y = shape[1] // 2
    tokens, width = forward_input.shape[1:]
    hidden = gate_weight.shape[1]
    topk = forward_routes.shape[2]
    vmem = pl.BlockSpec(memory_space=pltpu.VMEM)
    hbm = pl.BlockSpec(memory_space=pltpu.HBM)
    dma = pltpu.SemaphoreType.DMA

    def kernel(*refs):
        layer_kernel(shape, *refs)

    out = jax.ShapeDtypeStruct((tokens, width), BF16)
    next_rows, previous_rows = pl.pallas_call(
        kernel,
        out_shape=(out, out),
        in_specs=[hbm] * 11,
        out_specs=(vmem, vmem),
        scratch_shapes=[
            pltpu.VMEM((3, tokens, width), BF16),
            pltpu.VMEM((2, topk, tokens), jnp.int32),
            pltpu.VMEM((2, topk, tokens), F32),
            pltpu.VMEM((1, width), F32),
            pltpu.VMEM((3, hidden, width), BF16),
            pltpu.VMEM((3, EF, CAP, width), BF16),
            pltpu.VMEM((3, 2, n_y, CAP, width), BF16),
            pltpu.VMEM((EF * CAP, width), F32),
            pltpu.VMEM((EF * CAP, 128), F32),
            pltpu.VMEM((2, 2, n_y, CAP, width), F32),
            pltpu.VMEM((2, n_y, CAP, width), BF16),
            pltpu.VMEM((2, n_y, CAP, width), BF16),
            pltpu.VMEM((2, n_y, CAP, width), BF16),
            pltpu.VMEM((2, n_y, CAP, width), BF16),
            pltpu.VMEM((2, EF * CAP, width), BF16),
            pltpu.VMEM((2, EF * CAP, width), BF16),
            pltpu.VMEM((2, tokens, width), BF16),
            pltpu.VMEM((2, 2, tokens // 2, width), BF16),
            pltpu.VMEM((2, EF * CAP, tokens), BF16),
            pltpu.VMEM((2, EF * CAP, tokens), BF16),
            dma((11,)),
            dma((3, n_y)),
            dma((3, n_y)),
            dma((3, n_y)),
            dma((3, n_y)),
            dma((2, n_y)),
            dma((2, n_y)),
            dma((2, n_y)),
            dma((2, n_y)),
            dma((2, 2)),
            dma((2, 2)),
            dma((2, 2)),
            dma((2, 2)),
            dma((2,)),
            dma((2,)),
            dma((2,)),
            dma((2,)),
        ],
        compiler_params=pltpu.CompilerParams(
            collective_id=0, has_side_effects=True, vmem_limit_bytes=56 << 20
        ),
    )(
        forward_input[0],
        forward_routes[0].T,
        forward_shares[0].T,
        backward_input[0],
        backward_routes[0].T,
        backward_shares[0].T,
        output_grad[0],
        norm_gain,
        gate_weight[0],
        up_weight[0],
        down_weight[0],
    )
    return next_rows[None], previous_rows[None]


def solution(mesh):
    rows = P("section", "expert", None)
    in_specs = (rows,) * 7 + (P("section", None),) + (rows,) * 3
    return jax.shard_map(
        on_device, mesh=mesh, in_specs=in_specs, out_specs=(rows, rows), check_vma=False
    )
```
